32 devices in a mesh: ctx: 8 (over z, x), tp: 4 (over y, core).
Axes of the slice: x: 2, y: 2, z: 4, core: 2. Of those that a mesh axis runs over, the one named last changes fastest.
Arguments:
- tokens: bfloat16 [4096, 4096], P(('ctx', 'tp')), may hold values from -6 to 6
- in_weight: bfloat16 [4096, 3, 4096], P('ctx', None, 'tp'), may hold values from -0.09375 to 0.09375
- short_filter: float32 [3, 3, 4096], P(None, None, 'tp'), may hold values from -3 to 3
- decay_rates: float32 [16, 4096], P(None, 'tp'), may hold values from 1.2207031e-05 to 0.1, as said below
- residues: float32 [16, 4096], P(None, 'tp'), may hold values from -1.5 to 1.5
- skip_gain: float32 [4096], P('tp'), may hold values from -4 to 4
Outputs:
- mixed: bfloat16 [4096, 4096], P('ctx', 'tp')
The draws below stay inside these ranges and needn't reach their ends.
Inputs may be any that keep to these rules, and one draw needn't show every extreme that they name: `decay_rates`: positive decay rates.
All inputs are finite; a program needn't handle non-finite values.
Results may differ from the reference program's by a relative error of at most 0.0063.
Values may be sent and summed in bfloat16 or wider, within the bound.
A program may use at most 128 MiB of HBM per device.

```python
import jax
import jax.numpy as jnp
from jax import lax

D = 4096
MODES = 16
SHORT = 3
BLOCK = 32
SEQ = 4096


def draw_decay_rates(key, part):
    first, second, third = jax.random.split(key, 3)
    share = 0.5
    pick_slow = jax.random.uniform(first, (MODES, D), jnp.float32) < share
    slow_rates = jnp.exp(jax.random.uniform(second, (MODES, D), jnp.float32, jnp.log(0.05 / SEQ), jnp.log(2.0 / SEQ)))
    fast_rates = jnp.exp(jax.random.uniform(third, (MODES, D), jnp.float32, jnp.log(1.0 / 50.0), jnp.log(0.1)))
    return jnp.where(pick_slow, slow_rates, fast_rates).astype(jnp.float32)


def block_scale(rng, shape, shards, smallest, largest):
    gain = 1.0
    for position, shards_of in shards:
        steps = jax.random.uniform(jax.random.fold_in(jax.random.fold_in(rng, 6), position), (shards_of,), jnp.float32, smallest / len(shards), largest / len(shards))
        gain = gain * jnp.repeat(jnp.exp(steps), shape[position] // shards_of).reshape((-1,) + (1,) * (len(shape) - 1 - position))
    return gain


def scatter_about(stream_key, extent, width, bound, cuts=(), kind=jnp.bfloat16):
    array = jax.random.normal(stream_key, extent, jnp.float32) * width
    if len(cuts) > 0:
        array = block_scale(stream_key, extent, cuts, -0.22, 0.18) * array
    return jnp.clip(array, min=-bound, max=bound).astype(kind)


def setup_inputs(seed: int = 0) -> dict:
    arg_keys = jax.random.split(jax.random.key(seed), 7)
    return {
        "tokens": scatter_about(arg_keys[0], (SEQ, D), 1.0, 6.0, ((0, 32),)),
        "in_weight": scatter_about(arg_keys[1], (D, 3, D), D ** -0.5, 0.09375, ((0, 8), (2, 4))),
        "short_filter": scatter_about(arg_keys[2], (3, SHORT, D), 0.6, 3.0, ((2, 4),), jnp.float32),
        "decay_rates": draw_decay_rates(jax.random.fold_in(arg_keys[6], 71), 0),
        "residues": scatter_about(arg_keys[4], (MODES, D), 0.25, 1.5, ((1, 4),), jnp.float32),
        "skip_gain": scatter_about(arg_keys[5], (D,), 1.0, 4.0, ((0, 4),), jnp.float32),
    }


def block_scan(product, decay_rates, residues, block):
    channels = product.shape[1]
    mode_gain = residues * jnp.sqrt(2.0 * decay_rates)
    positions = jnp.arange(block, dtype=jnp.float32)
    kernel = lax.optimization_barrier(jnp.sum(mode_gain[None] * jnp.exp(-decay_rates[None] * positions[:, None, None]), axis=1))
    gaps = jnp.arange(block, dtype=jnp.int32)[:, None] - jnp.arange(block, dtype=jnp.int32)[None, :]
    toeplitz = jnp.where((gaps >= 0)[:, :, None], kernel[jnp.clip(gaps, 0, block - 1)], jnp.float32(0.0))
    read_out = mode_gain[None] * jnp.exp(-decay_rates[None] * (positions[:, None, None] + 1.0))
    take_in = jnp.exp(-decay_rates[None] * (block - 1.0 - positions)[:, None, None])
    step_decay = jnp.exp(-decay_rates * block)

    def advance(state, block_in):
        block_out = lax.optimization_barrier(jnp.sum(toeplitz * block_in[None], axis=1)) + lax.optimization_barrier(jnp.sum(read_out * state[None], axis=1))
        state = step_decay * state + lax.optimization_barrier(jnp.sum(take_in * block_in[:, None, :], axis=0))
        return (state, block_out)
    zero_state = jnp.zeros(decay_rates.shape, jnp.float32)
    state, outputs = lax.scan(advance, zero_state, product.reshape(-1, block, channels))
    return (outputs.reshape(-1, channels), state)

def reference(tokens, in_weight, short_filter, decay_rates, residues, skip_gain):
    projected = jnp.dot(tokens, in_weight.reshape(D, 3 * D), preferred_element_type=jnp.float32)
    projected = projected.astype(jnp.bfloat16).reshape(SEQ, 3, D)
    widened = jnp.pad(projected.astype(jnp.float32), ((SHORT - 1, 0), (0, 0), (0, 0)))
    features = jnp.zeros((SEQ, 3, D), jnp.float32)
    for offset in range(SHORT):
        features = features + short_filter[None, :, offset, :] * widened[SHORT - 1 - offset:SHORT - 1 - offset + SEQ]
    product = features[:, 1] * features[:, 2]
    inside, state = block_scan(product, decay_rates, residues, BLOCK)
    return (features[:, 0] * (inside + skip_gain[None] * product)).astype(jnp.bfloat16)
```

```python
import functools

import jax
import jax.numpy as jnp
from jax import lax
from jax.experimental import pallas as pl
from jax.experimental.pallas import tpu as pltpu
from jax.sharding import PartitionSpec as P

MESH = pl.DeviceIdType.MESH
VMEM_BYTES = 60 * 1024 * 1024
SUBLANES = 8
TAIL = 16
PIECES = 4
LANES = 128
ROWS = 128


def bits_of(count):
    bits, bit = [], count // 2
    while bit:
        bits.append(bit)
        bit //= 2
    return bits


def flipped(index, mask):
    bit = 1
    while bit <= mask:
        if mask & bit:
            index = index + bit - 2 * bit * ((index // bit) % 2)
        bit *= 2
    return index


def fused_kernel(Q, N, T, tok_ref, w_ref, filt_ref, dec_ref, res_ref, skip_ref, out_ref,
                 tok, w, wid, tail, halo, prod, consts, st, seg, allseg, outbuf,
                 tok_send, tok_recv, w_send, w_recv, halo_send, halo_recv, seg_send, seg_recv,
                 out_send, out_recv, own_sem):
    ctx, t = lax.axis_index("ctx"), lax.axis_index("tp")
    H = N // Q
    h, q = ctx // Q, ctx % Q
    R = tok.shape[2]
    G = tok_send.shape[1]
    part_rows = R // G
    L = T * R
    M = Q * L
    groups, branches, depth = w.shape[0], w.shape[1], w.shape[3]
    C = groups * LANES
    modes, lags = dec_ref.shape[0], filt_ref.shape[1]
    steps = M // SUBLANES

    def remote(src, dst, send, recv, device):
        return pltpu.make_async_remote_copy(
            src_ref=src, dst_ref=dst, send_sem=send, recv_sem=recv, device_id=device, device_id_type=MESH
        )

    def lanes(owner, g):
        return pl.ds(pl.multiple_of(owner * C + g * LANES, LANES), LANES)

    parts = []
    for g in range(groups):
        if g < groups - 1:
            parts.append((g, 0, branches))
        else:
            parts.append((g, 1, branches))
            parts.append((g, 0, 1))
    P_count = len(parts)

    own_tok = pltpu.make_async_copy(tok_ref, tok.at[q, t], own_sem.at[P_count])

    def own_w(p):
        g, lo, hi = parts[p]
        return pltpu.make_async_copy(w_ref.at[lo:hi, :, lanes(q, g)], w.at[g, lo:hi, ctx], own_sem.at[p])

    own_tok.start()
    for p in range(P_count):
        own_w(p).start()
    allseg[...] = jnp.zeros(allseg.shape, jnp.float32)

    barrier = pltpu.get_barrier_semaphore()
    for mask in range(1, N):
        pl.semaphore_signal(barrier, inc=1, device_id=(flipped(ctx, mask), t), device_id_type=MESH)
    for bit in bits_of(T):
        pl.semaphore_signal(barrier, inc=1, device_id=(ctx, flipped(t, bit)), device_id_type=MESH)
    pl.semaphore_wait(barrier, N - 1 + len(bits_of(T)))

    levels = [(bit, 0) for bit in bits_of(Q)] + [(0, bit) for bit in bits_of(T)]

    def source_of(m):
        qm = sum(levels[k][0] for k in range(len(levels)) if m >> k & 1)
        tm = sum(levels[k][1] for k in range(len(levels)) if m >> k & 1)
        return flipped(q, qm), flipped(t, tm)

    def piece(m, g):
        a, b = source_of(m)
        return tok.at[a, b, pl.ds(g * part_rows, part_rows)]

    def tok_copy(m, k, g):
        src = piece(m, g) if m else tok_ref.at[pl.ds(g * part_rows, part_rows)]
        to = m + (1 << k)
        return remote(
            src, piece(m, g), tok_send.at[to, g], tok_recv.at[to, g],
            (flipped(ctx, levels[k][0]), flipped(t, levels[k][1])),
        )

    def tok_arrived(m, g):
        ref = piece(m, g)
        remote(ref, ref, own_sem.at[0], tok_recv.at[m, g], (ctx, t)).wait_recv()

    def w_copy(to, p):
        g, lo, hi = parts[p]
        return remote(
            w_ref.at[lo:hi, :, lanes(to % Q, g)], w.at[g, lo:hi, ctx], w_send.at[to, p], w_recv.at[ctx, p], (to, t)
        )

    def w_arrived(mask, p):
        g, lo, hi = parts[p]
        source = flipped(ctx, mask)
        ref = w.at[g, lo:hi, source]
        if mask:
            remote(ref, ref, own_sem.at[0], w_recv.at[source, p], (ctx, t)).wait_recv()
        else:
            own_w(p).wait()

    top = Q // 2
    side = max(top, 1)
    near = [[m for m in range(Q, N) if m & top and (m % side > 0) == turn] for turn in (False, True)]
    far = [[m for m in range(Q, N) if not m & top and (m % side > 0) == turn] for turn in (False, True)]
    inside = [[m for m in range(1, Q) if m & top and (m % side > 0) == turn] for turn in (False, True)]
    beside = [m for m in range(1, Q) if not m & top]
    middle = (ctx // Q + ctx // side) % 2 == 1
    end = jnp.logical_not(middle)

    def send_w(masks, which, when=None):
        def act():
            for p in which:
                for mask in masks:
                    w_copy(flipped(ctx, mask), p).start()

        if when is None:
            act()
        else:
            pl.when(when)(act)

    def halo_copy(g, lo, hi):
        return remote(
            tail.at[g, lo:hi], halo.at[g, lo:hi], halo_send.at[g, lo], halo_recv.at[g, lo], (ctx + Q, t)
        )

    def seg_copy(g, d):
        return remote(seg.at[g], allseg.at[g, h], seg_send.at[g, d], seg_recv.at[g, h], (ctx + d * Q, t))

    def out_copy(g, s):
        return remote(
            outbuf.at[g, s], out_ref.at[:, lanes(q, g)], out_send.at[g, s], out_recv.at[g, q], (h * Q + s, t)
        )

    def own_out(g):
        return pltpu.make_async_copy(outbuf.at[g, q], out_ref.at[:, lanes(q, g)], own_sem.at[P_count + 1 + g])

    for g in range(G):
        for k in range(len(levels)):
            tok_copy(0, k, g).start()
    every = list(range(P_count))
    send_w(near[0]+inside[0]+near[1]+inside[1]+far[0]+far[1]+beside, every[:1], middle)
    send_w(far[0]+far[1]+near[0]+near[1]+inside[0]+inside[1]+beside, every[:1], end)

    dec = dec_ref[:, pl.ds(pl.multiple_of(q * C, LANES), C)]
    gain = res_ref[:, pl.ds(pl.multiple_of(q * C, LANES), C)] * jnp.sqrt(2.0 * dec)
    decay = jnp.exp(-dec)
    for m in range(modes):
        consts[0, m] = jnp.broadcast_to(decay[m : m + 1], (SUBLANES, C))
        consts[1, m] = jnp.broadcast_to(gain[m : m + 1], (SUBLANES, C))

    def forward(*some):
        for g in range(G):
            for m in some:
                tok_arrived(m, g)
                for k in range(m.bit_length(), len(levels)):
                    tok_copy(m, k, g).start()

    def by_hops(count):
        return sorted(range(count), key=lambda m: (bin(m).count("1"), m))

    def project_shard(g, lo, hi, s):
        a = tok.at[s].reshape(L, N * depth)
        b = [w.at[g, j].reshape(N * depth, LANES)[...] for j in range(lo, hi)]
        b = jnp.concatenate(b, axis=1) if len(b) > 1 else b[0]
        value = jnp.dot(a[...], b, preferred_element_type=jnp.float32)
        at = pl.ds(pl.multiple_of(SUBLANES + s * L, SUBLANES), L)
        for j in range(lo, hi):
            wid[j, at] = value[:, (j - lo) * LANES : (j - lo + 1) * LANES]

    def project_piece(g, lo, hi, part, first):
        b = [w.at[g, j, pl.ds(part * Q, Q)].reshape(Q * depth, LANES) for j in range(lo, hi)]

        @pl.loop(0, Q)
        def _(s):
            a = tok.at[s].reshape(L, N * depth)[:, pl.ds(pl.multiple_of(part * Q * depth, LANES), Q * depth)]
            c = [ref[...] for ref in b]
            c = jnp.concatenate(c, axis=1) if len(c) > 1 else c[0]
            value = jnp.dot(a, c, preferred_element_type=jnp.float32)
            at = pl.ds(pl.multiple_of(SUBLANES + s * L, SUBLANES), L)
            for j in range(lo, hi):
                add = value[:, (j - lo) * LANES : (j - lo + 1) * LANES]
                wid[j, at] = add if first else wid[j, at] + add

    def send_tail(g, lo, hi):
        for j in range(lo, hi):
            tail[g, j] = wid[j, SUBLANES + M - TAIL : SUBLANES + M].astype(jnp.bfloat16)

        @pl.when(h + 1 < H)
        def _():
            halo_copy(g, lo, hi).start()

    def take_halo(g, lo, hi):
        @pl.when(h == 0)
        def _():
            for j in range(lo, hi):
                wid[j, 0:SUBLANES] = jnp.zeros((SUBLANES, LANES), jnp.float32)

        @pl.when(h > 0)
        def _():
            if g == groups - 1:
                halo_copy(g, lo, hi).wait_recv()
            elif lo == 1:
                halo_copy(g, 0, branches).wait_recv()
            for j in range(lo, hi):
                wid[j, 0:SUBLANES] = halo[g, j].astype(jnp.float32)[TAIL - SUBLANES :]

    def features(g, j, start):
        block = wid[j, pl.ds(start, ROWS + SUBLANES)].astype(jnp.bfloat16).astype(jnp.float32)
        total = None
        for o in range(lags):
            term = filt_ref[j, o : o + 1, lanes(q, g)] * block[SUBLANES - o : SUBLANES - o + ROWS]
            total = term if total is None else total + term
        return total

    def convolve(g):
        @pl.loop(0, M // ROWS)
        def _(r):
            start = pl.multiple_of(r * ROWS, ROWS)
            prod[pl.ds(start, ROWS)] = features(g, 1, start) * features(g, 2, start)

        cols = slice(g * LANES, (g + 1) * LANES)
        factor = [consts[0, m, :, cols] for m in range(modes)]

        def gather(i, state):
            v = prod[pl.ds(i, SUBLANES, stride=steps), :]
            return tuple(f * s + v for f, s in zip(factor, state))

        zero = jnp.zeros((SUBLANES, LANES), jnp.float32)
        state = lax.fori_loop(0, steps, gather, (zero,) * modes, unroll=4)
        for m in range(modes):
            st[m] = state[m]
        rate = dec_ref[:, lanes(q, g)]
        sub_decay = jnp.exp(-rate * steps)
        e = jnp.zeros((modes, LANES), jnp.float32)
        for c in range(SUBLANES):
            e = sub_decay * e + st[:, c, :]
        seg[g] = e
        for d in range(1, H):
            @pl.when(h + d < H)
            def _():
                seg_copy(g, d).start()
        whole = jnp.exp(-rate * M)
        for d in range(H - 1):
            @pl.when(d < h)
            def _():
                ref = allseg.at[g, d]
                remote(ref, ref, own_sem.at[0], seg_recv.at[g, d], (ctx, t)).wait_recv()
        e = jnp.zeros((modes, LANES), jnp.float32)
        for d in range(H - 1):
            e = jnp.where(d < h, whole * e + allseg[g, d], e)
        for c in range(SUBLANES):
            now = st[:, c, :]
            st[:, c, :] = e
            e = sub_decay * e + now
        direct = jnp.broadcast_to(skip_ref[:, lanes(q, g)], (SUBLANES, LANES))

        def step(i, state):
            at = pl.ds(i, SUBLANES, stride=steps)
            v = prod[at, :]
            state = tuple(consts[0, m, :, cols] * s + v for m, s in enumerate(state))
            terms = [consts[1, m, :, cols] * s for m, s in enumerate(state)]
            terms.append(direct * v)
            while len(terms) > 1:
                terms = [a + b for a, b in zip(terms[::2], terms[1::2])] + (
                    [terms[-1]] if len(terms) % 2 else []
                )
            prod[at, :] = terms[0]
            return state

        lax.fori_loop(0, steps, step, tuple(st[m] for m in range(modes)), unroll=4)

    def finish(g):
        for s in range(Q - 1, -1, -1):
            if s == 0:
                take_halo(g, 0, 1)

            @pl.loop(0, L // ROWS)
            def _(r):
                start = pl.multiple_of(s * L + r * ROWS, ROWS)
                inner = pl.multiple_of(r * ROWS, ROWS)
                value = features(g, 0, start) * prod[pl.ds(start, ROWS)]
                outbuf[g, s, pl.ds(inner, ROWS)] = value.astype(outbuf.dtype)

            @pl.when(s != q)
            def _():
                out_copy(g, s).start()

            @pl.when(s == q)
            def _():
                own_out(g).start()

    forward(*[1 << k for k in range(len(bits_of(Q)))])
    send_w(near[0]+inside[0]+near[1]+inside[1]+far[0]+far[1]+beside, every[1:2], middle)
    send_w(far[0]+far[1]+near[0]+near[1]+inside[0]+inside[1]+beside, every[1:2], end)
    for m in by_hops(Q)[1:]:
        if m & (m - 1):
            forward(m)
    send_w(near[0]+inside[0]+near[1]+inside[1]+far[0]+far[1]+beside, every[2:], middle)
    send_w(far[0]+far[1]+near[0]+near[1]+inside[0]+inside[1]+beside, every[2:], end)
    for i, sm in enumerate(by_hops(Q)):
        for tm in by_hops(T)[1:]:
            forward(sm + Q * tm)
        if i == 0:
            own_tok.wait()
        if groups > 1:
            if i == 0:
                for mask in range(N):
                    w_arrived(mask, 0)
            shard = q
            for k, (bit, _) in enumerate(levels):
                if sm >> k & 1:
                    shard = flipped(shard, bit)
            project_shard(0, 1, branches, shard)
            project_shard(0, 0, 1, shard)
    for g in range(groups - 1):
        if g:
            for mask in range(N):
                w_arrived(mask, g)

            @pl.loop(0, Q)
            def _(s):
                project_shard(g, 1, branches, s)
                project_shard(g, 0, 1, s)
        send_tail(g, 0, branches)
        take_halo(g, 1, branches)
        convolve(g)
        finish(g)
    g = groups - 1
    for part in range(H):
        for mask in range(part * Q, part * Q + Q):
            w_arrived(mask, P_count - 2)
        project_piece(g, 1, branches, flipped(h, part), part == 0)
    send_tail(g, 1, branches)
    take_halo(g, 1, branches)
    convolve(g)
    for part in range(H):
        for mask in range(part * Q, part * Q + Q):
            w_arrived(mask, P_count - 1)
        project_piece(g, 0, 1, flipped(h, part), part == 0)
    send_tail(g, 0, 1)
    finish(g)

    for m in range(1 << len(levels)):
        for k in range(m.bit_length(), len(levels)):
            for g in range(G):
                tok_copy(m, k, g).wait_send()
    for p in range(P_count):
        for mask in range(1, N):
            w_copy(flipped(ctx, mask), p).wait_send()
    for g in range(groups):
        @pl.when(h + 1 < H)
        def _():
            if g < groups - 1:
                halo_copy(g, 0, branches).wait_send()
            else:
                halo_copy(g, 0, 1).wait_send()
                halo_copy(g, 1, branches).wait_send()
        for d in range(1, H):
            @pl.when(h + d < H)
            def _():
                seg_copy(g, d).wait_send()
        own_out(g).wait()
        for s in range(Q):
            @pl.when(s != q)
            def _():
                out_copy(g, s).wait_send()
                ref = out_ref.at[:, lanes(s, g)]
                remote(outbuf.at[g, s], ref, own_sem.at[0], out_recv.at[g, s], (ctx, t)).wait_recv()


def slices_of(count, token_bytes, weight_bytes, channels):
    best = None
    for Q in range(1, count):
        if count % Q or channels % (Q * LANES):
            continue
        cost = token_bytes * Q + 2 * weight_bytes // Q
        if best is None or cost < best[0]:
            best = (cost, Q)
    return best[1]


def per_device(tokens, in_weight, short_filter, decay_rates, residues, skip_gain):
    N, T = lax.axis_size("ctx"), lax.axis_size("tp")
    R, D = tokens.shape
    depth, branches, channels = in_weight.shape
    modes = decay_rates.shape[0]
    Q = slices_of(N, R * T * D, depth * N * branches * channels, channels)
    H = N // Q
    C = channels // Q
    L = R * T
    M = Q * L
    groups = C // LANES
    G = max(1, min(PIECES, R // TAIL))
    dma = pltpu.SemaphoreType.DMA
    hbm = pl.BlockSpec(memory_space=pl.ANY)
    vmem = pl.BlockSpec(memory_space=pltpu.VMEM)
    f32, bf16 = jnp.float32, jnp.bfloat16
    return pl.pallas_call(
        functools.partial(fused_kernel, Q, N, T),
        out_shape=jax.ShapeDtypeStruct((L, channels), bf16),
        in_specs=[hbm, hbm, vmem, vmem, vmem, vmem],
        out_specs=hbm,
        scratch_shapes=[
            pltpu.VMEM((Q, T, R, D), bf16),
            pltpu.VMEM((groups, branches, N, depth, LANES), bf16),
            pltpu.VMEM((branches, M + SUBLANES, LANES), f32),
            pltpu.VMEM((groups, branches, TAIL, LANES), bf16),
            pltpu.VMEM((groups, branches, TAIL, LANES), bf16),
            pltpu.VMEM((M, LANES), f32),
            pltpu.VMEM((2, modes, SUBLANES, C), f32),
            pltpu.VMEM((modes, SUBLANES, LANES), f32),
            pltpu.VMEM((groups, modes, LANES), f32),
            pltpu.VMEM((groups, H, modes, LANES), f32),
            pltpu.VMEM((groups, Q, L, LANES), bf16),
            dma((Q * T, G)), dma((Q * T, G)), dma((N, groups + 1)), dma((N, groups + 1)),
            dma((groups, 2)), dma((groups, 2)), dma((groups, H)), dma((groups, H)),
            dma((groups, Q)), dma((groups, Q)), dma((2 * groups + 2,)),
        ],
        compiler_params=pltpu.CompilerParams(
            collective_id=0, has_side_effects=True, vmem_limit_bytes=VMEM_BYTES
        ),
        name="project_and_filter",
    )(tokens, in_weight.transpose(1, 0, 2), short_filter, decay_rates, residues, skip_gain[None])


def solution(mesh):
    in_specs = (
        P(("ctx", "tp"), None),
        P("ctx", None, "tp"),
        P(None, None, "tp"),
        P(None, "tp"),
        P(None, "tp"),
        P("tp"),
    )
    return jax.shard_map(
        per_device, mesh=mesh, in_specs=in_specs, out_specs=P("ctx", "tp"), check_vma=False
    )
```

```python
import functools

import jax
import jax.numpy as jnp
from jax import lax
from jax.experimental import pallas as pl
from jax.experimental.pallas import tpu as pltpu
from jax.sharding import PartitionSpec as P

MESH = pl.DeviceIdType.MESH
VMEM_BYTES = 60 * 1024 * 1024
SUBLANES = 8
TAIL = 16
PIECES = 4
LANES = 128
ROWS = 128


def bits_of(count):
    bits, bit = [], count // 2
    while bit:
        bits.append(bit)
        bit //= 2
    return bits


def flipped(index, mask):
    bit = 1
    while bit <= mask:
        if mask & bit:
            index = index + bit - 2 * bit * ((index // bit) % 2)
        bit *= 2
    return index


def fused_kernel(Q, N, T, tok_ref, w_ref, filt_ref, dec_ref, res_ref, skip_ref, out_ref,
                 tok, w, wid, tail, halo, prod, consts, st, seg, allseg, outbuf,
                 tok_send, tok_recv, w_send, w_recv, halo_send, halo_recv, seg_send, seg_recv,
                 out_send, out_recv, own_sem):
    ctx, t = lax.axis_index("ctx"), lax.axis_index("tp")
    H = N // Q
    h, q = ctx // Q, ctx % Q
    R = tok.shape[2]
    G = tok_send.shape[1]
    part_rows = R // G
    L = T * R
    M = Q * L
    groups, branches, depth = w.shape[0], w.shape[1], w.shape[3]
    C = groups * LANES
    modes, lags = dec_ref.shape[0], filt_ref.shape[1]
    steps = M // SUBLANES

    def remote(src, dst, send, recv, device):
        return pltpu.make_async_remote_copy(
            src_ref=src, dst_ref=dst, send_sem=send, recv_sem=recv, device_id=device, device_id_type=MESH
        )

    def lanes(owner, g):
        return pl.ds(pl.multiple_of(owner * C + g * LANES, LANES), LANES)

    parts = []
    for g in range(groups):
        if g < groups - 1:
            parts.append((g, 0, branches))
        else:
            parts.append((g, 1, branches))
            parts.append((g, 0, 1))
    P_count = len(parts)

    own_tok = pltpu.make_async_copy(tok_ref, tok.at[q, t], own_sem.at[P_count])

    def own_w(p):
        g, lo, hi = parts[p]
        return pltpu.make_async_copy(w_ref.at[lo:hi, :, lanes(q, g)], w.at[g, lo:hi, ctx], own_sem.at[p])

    own_tok.start()
    for p in range(P_count):
        own_w(p).start()
    allseg[...] = jnp.zeros(allseg.shape, jnp.float32)

    barrier = pltpu.get_barrier_semaphore()
    for mask in range(1, N):
        pl.semaphore_signal(barrier, inc=1, device_id=(flipped(ctx, mask), t), device_id_type=MESH)
    for bit in bits_of(T):
        pl.semaphore_signal(barrier, inc=1, device_id=(ctx, flipped(t, bit)), device_id_type=MESH)
    pl.semaphore_wait(barrier, N - 1 + len(bits_of(T)))

    levels = [(bit, 0) for bit in bits_of(Q)] + [(0, bit) for bit in bits_of(T)]

    def source_of(m):
        qm = sum(levels[k][0] for k in range(len(levels)) if m >> k & 1)
        tm = sum(levels[k][1] for k in range(len(levels)) if m >> k & 1)
        return flipped(q, qm), flipped(t, tm)

    def piece(m, g):
        a, b = source_of(m)
        return tok.at[a, b, pl.ds(g * part_rows, part_rows)]

    def tok_copy(m, k, g):
        src = piece(m, g) if m else tok_ref.at[pl.ds(g * part_rows, part_rows)]
        to = m + (1 << k)
        return remote(
            src, piece(m, g), tok_send.at[to, g], tok_recv.at[to, g],
            (flipped(ctx, levels[k][0]), flipped(t, levels[k][1])),
        )

    def tok_arrived(m, g):
        ref = piece(m, g)
        remote(ref, ref, own_sem.at[0], tok_recv.at[m, g], (ctx, t)).wait_recv()

    def w_copy(to, p):
        g, lo, hi = parts[p]
        return remote(
            w_ref.at[lo:hi, :, lanes(to % Q, g)], w.at[g, lo:hi, ctx], w_send.at[to, p], w_recv.at[ctx, p], (to, t)
        )

    def w_arrived(mask, p):
        g, lo, hi = parts[p]
        source = flipped(ctx, mask)
        ref = w.at[g, lo:hi, source]
        if mask:
            remote(ref, ref, own_sem.at[0], w_recv.at[source, p], (ctx, t)).wait_recv()
        else:
            own_w(p).wait()

    top = Q // 2
    side = max(top, 1)
    near = [[m for m in range(Q, N) if m & top and (m % side > 0) == turn] for turn in (False, True)]
    far = [[m for m in range(Q, N) if not m & top and (m % side > 0) == turn] for turn in (False, True)]
    inside = [[m for m in range(1, Q) if m & top and (m % side > 0) == turn] for turn in (False, True)]
    beside = [m for m in range(1, Q) if not m & top]
    middle = (ctx // Q + ctx // side) % 2 == 1
    end = jnp.logical_not(middle)

    from_middle = near[0] + inside[0] + near[1] + inside[1] + far[0] + far[1] + beside
    from_end = far[0] + far[1] + near[0] + near[1] + inside[0] + inside[1] + beside

    def send_w(p, inner=(True, False)):
        for here, masks in ((middle, from_middle), (end, from_end)):
            @pl.when(here)
            def _():
                for mask in masks:
                    if (mask < Q) in inner:
                        w_copy(flipped(ctx, mask), p).start()

    def halo_copy(g, lo, hi):
        return remote(
            tail.at[g, lo:hi], halo.at[g, lo:hi], halo_send.at[g, lo], halo_recv.at[g, lo], (ctx + Q, t)
        )

    def seg_copy(g, d):
        return remote(seg.at[g], allseg.at[g, h], seg_send.at[g, d], seg_recv.at[g, h], (ctx + d * Q, t))

    def out_copy(g, s):
        return remote(
            outbuf.at[g, s], out_ref.at[:, lanes(q, g)], out_send.at[g, s], out_recv.at[g, q], (h * Q + s, t)
        )

    def own_out(g):
        return pltpu.make_async_copy(outbuf.at[g, q], out_ref.at[:, lanes(q, g)], own_sem.at[P_count + 1 + g])

    for g in range(G):
        for k in range(len(levels)):
            tok_copy(0, k, g).start()
    send_w(0)

    dec = dec_ref[:, pl.ds(pl.multiple_of(q * C, LANES), C)]
    gain = res_ref[:, pl.ds(pl.multiple_of(q * C, LANES), C)] * jnp.sqrt(2.0 * dec)
    decay = jnp.exp(-dec)
    for m in range(modes):
        consts[0, m] = jnp.broadcast_to(decay[m : m + 1], (SUBLANES, C))
        consts[1, m] = jnp.broadcast_to(gain[m : m + 1], (SUBLANES, C))

    def forward(*some, pieces=range(G)):
        for g in pieces:
            for m in some:
                tok_arrived(m, g)
                for k in range(m.bit_length(), len(levels)):
                    tok_copy(m, k, g).start()

    def by_hops(count):
        return sorted(range(count), key=lambda m: (bin(m).count("1"), m))

    def rounded(value):
        return value.astype(jnp.bfloat16).astype(jnp.float32)

    def project_shard(g, lo, hi, s):
        a = tok.at[s].reshape(L, N * depth)
        b = [w.at[g, j].reshape(N * depth, LANES)[...] for j in range(lo, hi)]
        b = jnp.concatenate(b, axis=1) if len(b) > 1 else b[0]
        value = jnp.dot(a[...], b, preferred_element_type=jnp.float32)
        at = pl.ds(pl.multiple_of(SUBLANES + s * L, SUBLANES), L)
        for j in range(lo, hi):
            wid[j, at] = rounded(value[:, (j - lo) * LANES : (j - lo + 1) * LANES])

    def project_piece(g, lo, hi, part, first, last):
        b = [w.at[g, j, pl.ds(part * Q, Q)].reshape(Q * depth, LANES) for j in range(lo, hi)]

        @pl.loop(0, Q)
        def _(s):
            a = tok.at[s].reshape(L, N * depth)[:, pl.ds(pl.multiple_of(part * Q * depth, LANES), Q * depth)]
            c = [ref[...] for ref in b]
            c = jnp.concatenate(c, axis=1) if len(c) > 1 else c[0]
            value = jnp.dot(a, c, preferred_element_type=jnp.float32)
            at = pl.ds(pl.multiple_of(SUBLANES + s * L, SUBLANES), L)
            for j in range(lo, hi):
                add = value[:, (j - lo) * LANES : (j - lo + 1) * LANES]
                add = add if first else wid[j, at] + add
                wid[j, at] = rounded(add) if last else add

    def send_tail(g, lo, hi):
        for j in range(lo, hi):
            tail[g, j] = wid[j, SUBLANES + M - TAIL : SUBLANES + M].astype(jnp.bfloat16)

        @pl.when(h + 1 < H)
        def _():
            halo_copy(g, lo, hi).start()

    def take_halo(g, lo, hi):
        @pl.when(h == 0)
        def _():
            for j in range(lo, hi):
                wid[j, 0:SUBLANES] = jnp.zeros((SUBLANES, LANES), jnp.float32)

        @pl.when(h > 0)
        def _():
            if g == groups - 1:
                halo_copy(g, lo, hi).wait_recv()
            elif lo == 1:
                halo_copy(g, 0, branches).wait_recv()
            for j in range(lo, hi):
                wid[j, 0:SUBLANES] = halo[g, j].astype(jnp.float32)[TAIL - SUBLANES :]

    def features(g, j, start):
        total = None
        for o in range(lags):
            term = filt_ref[j, o : o + 1, lanes(q, g)] * wid[j, pl.ds(start + (SUBLANES - o), ROWS)]
            total = term if total is None else total + term
        return total

    def gather_states(g):
        @pl.loop(0, M // ROWS)
        def _(r):
            start = pl.multiple_of(r * ROWS, ROWS)
            prod[pl.ds(start, ROWS)] = features(g, 1, start) * features(g, 2, start)

        cols = slice(g * LANES, (g + 1) * LANES)
        factor = [consts[0, m, :, cols] for m in range(modes)]

        def gather(i, state):
            v = prod[pl.ds(i, SUBLANES, stride=steps), :]
            return tuple(f * s + v for f, s in zip(factor, state))

        zero = jnp.zeros((SUBLANES, LANES), jnp.float32)
        state = lax.fori_loop(0, steps, gather, (zero,) * modes, unroll=4)
        for m in range(modes):
            st[m] = state[m]
        rate = dec_ref[:, lanes(q, g)]
        sub_decay = jnp.exp(-rate * steps)
        e = jnp.zeros((modes, LANES), jnp.float32)
        for c in range(SUBLANES):
            e = sub_decay * e + st[:, c, :]
        seg[g] = e
        for d in range(1, H):
            @pl.when(h + d < H)
            def _():
                seg_copy(g, d).start()

    def convolve(g):
        cols = slice(g * LANES, (g + 1) * LANES)
        rate = dec_ref[:, lanes(q, g)]
        sub_decay = jnp.exp(-rate * steps)
        whole = jnp.exp(-rate * M)
        for d in range(H - 1):
            @pl.when(d < h)
            def _():
                ref = allseg.at[g, d]
                remote(ref, ref, own_sem.at[0], seg_recv.at[g, d], (ctx, t)).wait_recv()
        e = jnp.zeros((modes, LANES), jnp.float32)
        for d in range(H - 1):
            e = jnp.where(d < h, whole * e + allseg[g, d], e)
        for c in range(SUBLANES):
            now = st[:, c, :]
            st[:, c, :] = e
            e = sub_decay * e + now
        direct = jnp.broadcast_to(skip_ref[:, lanes(q, g)], (SUBLANES, LANES))

        def step(i, state):
            at = pl.ds(i, SUBLANES, stride=steps)
            v = prod[at, :]
            state = tuple(consts[0, m, :, cols] * s + v for m, s in enumerate(state))
            terms = [consts[1, m, :, cols] * s for m, s in enumerate(state)]
            terms.append(direct * v)
            while len(terms) > 1:
                terms = [a + b for a, b in zip(terms[::2], terms[1::2])] + (
                    [terms[-1]] if len(terms) % 2 else []
                )
            prod[at, :] = terms[0]
            return state

        lax.fori_loop(0, steps, step, tuple(st[m] for m in range(modes)), unroll=4)

    def finish(g):
        for s in range(Q - 1, -1, -1):
            if s == 0:
                take_halo(g, 0, 1)

            @pl.loop(0, L // ROWS)
            def _(r):
                start = pl.multiple_of(s * L + r * ROWS, ROWS)
                inner = pl.multiple_of(r * ROWS, ROWS)
                value = features(g, 0, start) * prod[pl.ds(start, ROWS)]
                outbuf[g, s, pl.ds(inner, ROWS)] = value.astype(outbuf.dtype)

            @pl.when(s != q)
            def _():
                out_copy(g, s).start()

            @pl.when(s == q)
            def _():
                own_out(g).start()

    last = groups - 1
    shards = by_hops(Q)
    forward(*[m for m in shards if bin(m).count("1") == 1])
    if P_count > 1:
        send_w(1)
    early = shards[:-1] if Q > 2 else shards
    late = shards[len(early) :]
    half = G // 2 if late else 0
    for m in shards:
        if m & (m - 1):
            forward(m, pieces=range(half))
    for sm in early:
        for tm in by_hops(T)[1:]:
            forward(sm + Q * tm)
    for m in shards:
        if m & (m - 1):
            forward(m, pieces=range(half, G))
    own_tok.wait()

    def project_first(sm):
        shard = q
        for k, (bit, _) in enumerate(levels):
            if sm >> k & 1:
                shard = flipped(shard, bit)
        project_shard(0, 1, branches, shard)
        project_shard(0, 0, 1, shard)

    if last:
        for mask in range(N):
            w_arrived(mask, 0)
        for sm in early:
            project_first(sm)
    for sm in late:
        for tm in by_hops(T)[1:]:
            forward(sm + Q * tm)
        if last:
            project_first(sm)

    for p in range(2, P_count):
        send_w(p, (True,))

    def project_last(p, part):
        for mask in range(part * Q, part * Q + Q):
            w_arrived(mask, p)
        g, lo, hi = parts[p]
        project_piece(g, lo, hi, flipped(h, part), part == 0, part == H - 1)

    for g in range(last):
        if g:
            for mask in range(N):
                w_arrived(mask, g)

            @pl.loop(0, Q)
            def _(s):
                project_shard(g, 1, branches, s)
                project_shard(g, 0, 1, s)
        send_tail(g, 0, branches)
        take_halo(g, 1, branches)
        gather_states(g)
        if g == last - 1:
            project_last(P_count - 2, 0)
        convolve(g)
        finish(g)
    for p in range(2, P_count):
        send_w(p, (False,))
    for part in range(1 if last else 0, H):
        project_last(P_count - 2, part)
    send_tail(last, 1, branches)
    take_halo(last, 1, branches)
    gather_states(last)
    project_last(P_count - 1, 0)
    convolve(last)
    for part in range(1, H):
        project_last(P_count - 1, part)
    send_tail(last, 0, 1)
    finish(last)

    for m in range(1 << len(levels)):
        for k in range(m.bit_length(), len(levels)):
            for g in range(G):
                tok_copy(m, k, g).wait_send()
    for p in range(P_count):
        for mask in range(1, N):
            w_copy(flipped(ctx, mask), p).wait_send()
    for g in range(groups):
        @pl.when(h + 1 < H)
        def _():
            if g < groups - 1:
                halo_copy(g, 0, branches).wait_send()
            else:
                halo_copy(g, 0, 1).wait_send()
                halo_copy(g, 1, branches).wait_send()
        for d in range(1, H):
            @pl.when(h + d < H)
            def _():
                seg_copy(g, d).wait_send()
        own_out(g).wait()
        for s in range(Q):
            @pl.when(s != q)
            def _():
                out_copy(g, s).wait_send()
                ref = out_ref.at[:, lanes(s, g)]
                remote(outbuf.at[g, s], ref, own_sem.at[0], out_recv.at[g, s], (ctx, t)).wait_recv()


def slices_of(count, token_bytes, weight_bytes, channels):
    best = None
    for Q in range(1, count):
        if count % Q or channels % (Q * LANES):
            continue
        cost = token_bytes * Q + 2 * weight_bytes // Q
        if best is None or cost < best[0]:
            best = (cost, Q)
    return best[1]


def per_device(tokens, in_weight, short_filter, decay_rates, residues, skip_gain):
    N, T = lax.axis_size("ctx"), lax.axis_size("tp")
    R, D = tokens.shape
    depth, branches, channels = in_weight.shape
    modes = decay_rates.shape[0]
    Q = slices_of(N, R * T * D, depth * N * branches * channels, channels)
    H = N // Q
    C = channels // Q
    L = R * T
    M = Q * L
    groups = C // LANES
    G = max(1, min(PIECES, R // TAIL))
    dma = pltpu.SemaphoreType.DMA
    hbm = pl.BlockSpec(memory_space=pl.ANY)
    vmem = pl.BlockSpec(memory_space=pltpu.VMEM)
    f32, bf16 = jnp.float32, jnp.bfloat16
    return pl.pallas_call(
        functools.partial(fused_kernel, Q, N, T),
        out_shape=jax.ShapeDtypeStruct((L, channels), bf16),
        in_specs=[hbm, hbm, vmem, vmem, vmem, vmem],
        out_specs=hbm,
        scratch_shapes=[
            pltpu.VMEM((Q, T, R, D), bf16),
            pltpu.VMEM((groups, branches, N, depth, LANES), bf16),
            pltpu.VMEM((branches, M + SUBLANES, LANES), f32),
            pltpu.VMEM((groups, branches, TAIL, LANES), bf16),
            pltpu.VMEM((groups, branches, TAIL, LANES), bf16),
            pltpu.VMEM((M, LANES), f32),
            pltpu.VMEM((2, modes, SUBLANES, C), f32),
            pltpu.VMEM((modes, SUBLANES, LANES), f32),
            pltpu.VMEM((groups, modes, LANES), f32),
            pltpu.VMEM((groups, H, modes, LANES), f32),
            pltpu.VMEM((groups, Q, L, LANES), bf16),
            dma((Q * T, G)), dma((Q * T, G)), dma((N, groups + 1)), dma((N, groups + 1)),
            dma((groups, 2)), dma((groups, 2)), dma((groups, H)), dma((groups, H)),
            dma((groups, Q)), dma((groups, Q)), dma((2 * groups + 2,)),
        ],
        compiler_params=pltpu.CompilerParams(
            collective_id=0, has_side_effects=True, vmem_limit_bytes=VMEM_BYTES
        ),
        name="project_and_filter",
    )(tokens, in_weight.transpose(1, 0, 2), short_filter, decay_rates, residues, skip_gain[None])


def solution(mesh):
    in_specs = (
        P(("ctx", "tp"), None),
        P("ctx", None, "tp"),
        P(None, None, "tp"),
        P(None, "tp"),
        P(None, "tp"),
        P("tp"),
    )
    return jax.shard_map(
        per_device, mesh=mesh, in_specs=in_specs, out_specs=P("ctx", "tp"), check_vma=False
    )
```

```python
import functools

import jax
import jax.numpy as jnp
from jax import lax
from jax.experimental import pallas as pl
from jax.experimental.pallas import tpu as pltpu
from jax.sharding import PartitionSpec as P

MESH = pl.DeviceIdType.MESH
VMEM_BYTES = 60 * 1024 * 1024
SUBLANES = 8
TAIL = 16
PIECES = 2
LANES = 128
ROWS = 128


def bits_of(count):
    bits, bit = [], count // 2
    while bit:
        bits.append(bit)
        bit //= 2
    return bits


def flipped(index, mask):
    bit = 1
    while bit <= mask:
        if mask & bit:
            index = index + bit - 2 * bit * ((index // bit) % 2)
        bit *= 2
    return index


def fused_kernel(Q, N, T, tok_ref, w_ref, filt_ref, dec_ref, res_ref, skip_ref, out_ref,
                 tok, w, wid, tail, halo, prod, consts, st, seg, allseg, outbuf,
                 tok_send, tok_recv, w_send, w_recv, halo_send, halo_recv, seg_send, seg_recv,
                 out_send, out_recv, own_sem):
    ctx, t = lax.axis_index("ctx"), lax.axis_index("tp")
    H = N // Q
    h, q = ctx // Q, ctx % Q
    R = tok.shape[2]
    G = tok_send.shape[1]
    part_rows = R // G
    L = T * R
    M = Q * L
    groups, branches, depth = w.shape[0], w.shape[1], w.shape[3]
    C = groups * LANES
    modes, lags = dec_ref.shape[0], filt_ref.shape[1]
    steps = M // SUBLANES

    def remote(src, dst, send, recv, device):
        return pltpu.make_async_remote_copy(
            src_ref=src, dst_ref=dst, send_sem=send, recv_sem=recv, device_id=device, device_id_type=MESH
        )

    def lanes(owner, g):
        return pl.ds(pl.multiple_of(owner * C + g * LANES, LANES), LANES)

    parts = []
    for g in range(groups):
        if g < groups - 1:
            parts.append((g, 0, branches))
        else:
            parts.append((g, 1, branches))
            parts.append((g, 0, 1))
    P_count = len(parts)

    own_tok = pltpu.make_async_copy(tok_ref, tok.at[q, t], own_sem.at[P_count])

    def own_w(p):
        g, lo, hi = parts[p]
        return pltpu.make_async_copy(w_ref.at[lo:hi, :, lanes(q, g)], w.at[g, lo:hi, ctx], own_sem.at[p])

    own_tok.start()
    for p in range(P_count):
        own_w(p).start()
    allseg[...] = jnp.zeros(allseg.shape, jnp.float32)

    barrier = pltpu.get_barrier_semaphore()
    for mask in range(1, N):
        pl.semaphore_signal(barrier, inc=1, device_id=(flipped(ctx, mask), t), device_id_type=MESH)
    for bit in bits_of(T):
        pl.semaphore_signal(barrier, inc=1, device_id=(ctx, flipped(t, bit)), device_id_type=MESH)
    pl.semaphore_wait(barrier, N - 1 + len(bits_of(T)))

    levels = [(bit, 0) for bit in bits_of(Q)] + [(0, bit) for bit in bits_of(T)]

    def source_of(m):
        qm = sum(levels[k][0] for k in range(len(levels)) if m >> k & 1)
        tm = sum(levels[k][1] for k in range(len(levels)) if m >> k & 1)
        return flipped(q, qm), flipped(t, tm)

    def piece(m, g):
        a, b = source_of(m)
        return tok.at[a, b, pl.ds(g * part_rows, part_rows)]

    def tok_copy(m, k, g):
        src = piece(m, g) if m else tok_ref.at[pl.ds(g * part_rows, part_rows)]
        to = m + (1 << k)
        return remote(
            src, piece(m, g), tok_send.at[to, g], tok_recv.at[to, g],
            (flipped(ctx, levels[k][0]), flipped(t, levels[k][1])),
        )

    def tok_arrived(m, g):
        ref = piece(m, g)
        remote(ref, ref, own_sem.at[0], tok_recv.at[m, g], (ctx, t)).wait_recv()

    def w_copy(to, p):
        g, lo, hi = parts[p]
        return remote(
            w_ref.at[lo:hi, :, lanes(to % Q, g)], w.at[g, lo:hi, ctx], w_send.at[to, p], w_recv.at[ctx, p], (to, t)
        )

    def w_arrived(mask, p):
        g, lo, hi = parts[p]
        source = flipped(ctx, mask)
        ref = w.at[g, lo:hi, source]
        if mask:
            remote(ref, ref, own_sem.at[0], w_recv.at[source, p], (ctx, t)).wait_recv()
        else:
            own_w(p).wait()

    top = Q // 2
    side = max(top, 1)
    near = [[m for m in range(Q, N) if m & top and (m % side > 0) == turn] for turn in (False, True)]
    far = [[m for m in range(Q, N) if not m & top and (m % side > 0) == turn] for turn in (False, True)]
    inside = [[m for m in range(1, Q) if m & top and (m % side > 0) == turn] for turn in (False, True)]
    beside = [m for m in range(1, Q) if not m & top]
    middle = (ctx // Q + ctx // side) % 2 == 1
    end = jnp.logical_not(middle)

    from_middle = near[0] + inside[0] + near[1] + inside[1] + far[0] + far[1] + beside
    from_end = far[0] + far[1] + near[0] + near[1] + inside[0] + inside[1] + beside

    def send_w(p, inner=(True, False)):
        for here, masks in ((middle, from_middle), (end, from_end)):
            @pl.when(here)
            def _():
                for mask in masks:
                    if (mask < Q) in inner:
                        w_copy(flipped(ctx, mask), p).start()

    def halo_copy(g, lo, hi):
        return remote(
            tail.at[g, lo:hi], halo.at[g, lo:hi], halo_send.at[g, lo], halo_recv.at[g, lo], (ctx + Q, t)
        )

    def seg_copy(g, d):
        return remote(seg.at[g], allseg.at[g, h], seg_send.at[g, d], seg_recv.at[g, h], (ctx + d * Q, t))

    def out_copy(g, s):
        return remote(
            outbuf.at[g, s], out_ref.at[:, lanes(q, g)], out_send.at[g, s], out_recv.at[g, q], (h * Q + s, t)
        )

    def own_out(g):
        return pltpu.make_async_copy(outbuf.at[g, q], out_ref.at[:, lanes(q, g)], own_sem.at[P_count + 1 + g])

    for g in range(G):
        for k in range(len(levels)):
            tok_copy(0, k, g).start()
    send_w(0)

    dec = dec_ref[:, pl.ds(pl.multiple_of(q * C, LANES), C)]
    gain = res_ref[:, pl.ds(pl.multiple_of(q * C, LANES), C)] * jnp.sqrt(2.0 * dec)
    decay = jnp.exp(-dec)
    for m in range(modes):
        consts[0, m] = jnp.broadcast_to(decay[m : m + 1], (SUBLANES, C))
        consts[1, m] = jnp.broadcast_to(gain[m : m + 1], (SUBLANES, C))

    def forward(*some, pieces=range(G)):
        for g in pieces:
            for m in some:
                tok_arrived(m, g)
                for k in range(m.bit_length(), len(levels)):
                    tok_copy(m, k, g).start()

    def by_hops(count):
        return sorted(range(count), key=lambda m: (bin(m).count("1"), m))

    def rounded(value):
        return value.astype(jnp.bfloat16).astype(jnp.float32)

    def project_shard(g, lo, hi, s):
        a = tok.at[s].reshape(L, N * depth)
        b = [w.at[g, j].reshape(N * depth, LANES)[...] for j in range(lo, hi)]
        b = jnp.concatenate(b, axis=1) if len(b) > 1 else b[0]
        value = jnp.dot(a[...], b, preferred_element_type=jnp.float32)
        at = pl.ds(pl.multiple_of(SUBLANES + s * L, SUBLANES), L)
        for j in range(lo, hi):
            wid[j, at] = rounded(value[:, (j - lo) * LANES : (j - lo + 1) * LANES])

    def project_piece(g, lo, hi, part, first, last):
        b = [w.at[g, j, pl.ds(part * Q, Q)].reshape(Q * depth, LANES) for j in range(lo, hi)]

        @pl.loop(0, Q)
        def _(s):
            a = tok.at[s].reshape(L, N * depth)[:, pl.ds(pl.multiple_of(part * Q * depth, LANES), Q * depth)]
            c = [ref[...] for ref in b]
            c = jnp.concatenate(c, axis=1) if len(c) > 1 else c[0]
            value = jnp.dot(a, c, preferred_element_type=jnp.float32)
            at = pl.ds(pl.multiple_of(SUBLANES + s * L, SUBLANES), L)
            for j in range(lo, hi):
                add = value[:, (j - lo) * LANES : (j - lo + 1) * LANES]
                add = add if first else wid[j, at] + add
                wid[j, at] = rounded(add) if last else add

    def send_tail(g, lo, hi):
        for j in range(lo, hi):
            tail[g, j] = wid[j, SUBLANES + M - TAIL : SUBLANES + M].astype(jnp.bfloat16)

        @pl.when(h + 1 < H)
        def _():
            halo_copy(g, lo, hi).start()

    def take_halo(g, lo, hi):
        @pl.when(h == 0)
        def _():
            for j in range(lo, hi):
                wid[j, 0:SUBLANES] = jnp.zeros((SUBLANES, LANES), jnp.float32)

        @pl.when(h > 0)
        def _():
            if g == groups - 1:
                halo_copy(g, lo, hi).wait_recv()
            elif lo == 1:
                halo_copy(g, 0, branches).wait_recv()
            for j in range(lo, hi):
                wid[j, 0:SUBLANES] = halo[g, j].astype(jnp.float32)[TAIL - SUBLANES :]

    def features(g, j, start):
        total = None
        for o in range(lags):
            term = filt_ref[j, o : o + 1, lanes(q, g)] * wid[j, pl.ds(start + (SUBLANES - o), ROWS)]
            total = term if total is None else total + term
        return total

    def gather_states(g):
        @pl.loop(0, M // ROWS)
        def _(r):
            start = pl.multiple_of(r * ROWS, ROWS)
            prod[pl.ds(start, ROWS)] = features(g, 1, start) * features(g, 2, start)

        cols = slice(g * LANES, (g + 1) * LANES)
        factor = [consts[0, m, :, cols] for m in range(modes)]

        def gather(i, state):
            v = prod[pl.ds(i, SUBLANES, stride=steps), :]
            return tuple(f * s + v for f, s in zip(factor, state))

        zero = jnp.zeros((SUBLANES, LANES), jnp.float32)
        state = lax.fori_loop(0, steps, gather, (zero,) * modes, unroll=8)
        for m in range(modes):
            st[m] = state[m]
        rate = dec_ref[:, lanes(q, g)]
        sub_decay = jnp.exp(-rate * steps)
        e = jnp.zeros((modes, LANES), jnp.float32)
        for c in range(SUBLANES):
            e = sub_decay * e + st[:, c, :]
        seg[g] = e
        for d in range(1, H):
            @pl.when(h + d < H)
            def _():
                seg_copy(g, d).start()

    def convolve(g):
        cols = slice(g * LANES, (g + 1) * LANES)
        rate = dec_ref[:, lanes(q, g)]
        sub_decay = jnp.exp(-rate * steps)
        whole = jnp.exp(-rate * M)
        for d in range(H - 1):
            @pl.when(d < h)
            def _():
                ref = allseg.at[g, d]
                remote(ref, ref, own_sem.at[0], seg_recv.at[g, d], (ctx, t)).wait_recv()
        e = jnp.zeros((modes, LANES), jnp.float32)
        for d in range(H - 1):
            e = jnp.where(d < h, whole * e + allseg[g, d], e)
        for c in range(SUBLANES):
            now = st[:, c, :]
            st[:, c, :] = e
            e = sub_decay * e + now
        direct = jnp.broadcast_to(skip_ref[:, lanes(q, g)], (SUBLANES, LANES))

        def step(i, state):
            at = pl.ds(i, SUBLANES, stride=steps)
            v = prod[at, :]
            state = tuple(consts[0, m, :, cols] * s + v for m, s in enumerate(state))
            terms = [consts[1, m, :, cols] * s for m, s in enumerate(state)]
            terms.append(direct * v)
            while len(terms) > 1:
                terms = [a + b for a, b in zip(terms[::2], terms[1::2])] + (
                    [terms[-1]] if len(terms) % 2 else []
                )
            prod[at, :] = terms[0]
            return state

        lax.fori_loop(0, steps, step, tuple(st[m] for m in range(modes)), unroll=8)

    def finish(g):
        for s in range(Q - 1, -1, -1):
            if s == 0:
                take_halo(g, 0, 1)

            @pl.loop(0, L // ROWS)
            def _(r):
                start = pl.multiple_of(s * L + r * ROWS, ROWS)
                inner = pl.multiple_of(r * ROWS, ROWS)
                value = features(g, 0, start) * prod[pl.ds(start, ROWS)]
                outbuf[g, s, pl.ds(inner, ROWS)] = value.astype(outbuf.dtype)

            @pl.when(s != q)
            def _():
                out_copy(g, s).start()

            @pl.when(s == q)
            def _():
                own_out(g).start()

    last = groups - 1
    shards = by_hops(Q)
    forward(*[m for m in shards if bin(m).count("1") == 1])
    if P_count > 1:
        send_w(1)
    early = shards[:-1] if Q > 2 else shards
    late = shards[len(early) :]
    half = G // 2 if late else 0
    for m in shards:
        if m & (m - 1):
            forward(m, pieces=range(half))
    for sm in early:
        for tm in by_hops(T)[1:]:
            forward(sm + Q * tm)
    for m in shards:
        if m & (m - 1):
            forward(m, pieces=range(half, G))
    own_tok.wait()

    def project_first(sm):
        shard = q
        for k, (bit, _) in enumerate(levels):
            if sm >> k & 1:
                shard = flipped(shard, bit)
        project_shard(0, 1, branches, shard)
        project_shard(0, 0, 1, shard)

    if last:
        for mask in range(N):
            w_arrived(mask, 0)
        for sm in early:
            project_first(sm)
    for sm in late:
        for tm in by_hops(T)[1:]:
            forward(sm + Q * tm)
        if last:
            project_first(sm)

    for p in range(2, P_count):
        send_w(p, (True,))

    def project_last(p, part):
        for mask in range(part * Q, part * Q + Q):
            w_arrived(mask, p)
        g, lo, hi = parts[p]
        project_piece(g, lo, hi, flipped(h, part), part == 0, part == H - 1)

    for g in range(last):
        if g:
            for mask in range(N):
                w_arrived(mask, g)

            @pl.loop(0, Q)
            def _(s):
                project_shard(g, 1, branches, s)
                project_shard(g, 0, 1, s)
        send_tail(g, 0, branches)
        take_halo(g, 1, branches)
        gather_states(g)
        if g == last - 1:
            project_last(P_count - 2, 0)
        convolve(g)
        finish(g)
    for p in range(2, P_count):
        send_w(p, (False,))
    for part in range(1 if last else 0, H):
        project_last(P_count - 2, part)
    send_tail(last, 1, branches)
    take_halo(last, 1, branches)
    gather_states(last)
    project_last(P_count - 1, 0)
    convolve(last)
    for part in range(1, H):
        project_last(P_count - 1, part)
    send_tail(last, 0, 1)
    finish(last)

    for m in range(1 << len(levels)):
        for k in range(m.bit_length(), len(levels)):
            for g in range(G):
                tok_copy(m, k, g).wait_send()
    for p in range(P_count):
        for mask in range(1, N):
            w_copy(flipped(ctx, mask), p).wait_send()
    for g in range(groups):
        @pl.when(h + 1 < H)
        def _():
            if g < groups - 1:
                halo_copy(g, 0, branches).wait_send()
            else:
                halo_copy(g, 0, 1).wait_send()
                halo_copy(g, 1, branches).wait_send()
        for d in range(1, H):
            @pl.when(h + d < H)
            def _():
                seg_copy(g, d).wait_send()
        own_out(g).wait()
        for s in range(Q):
            @pl.when(s != q)
            def _():
                out_copy(g, s).wait_send()
                ref = out_ref.at[:, lanes(s, g)]
                remote(outbuf.at[g, s], ref, own_sem.at[0], out_recv.at[g, s], (ctx, t)).wait_recv()


def slices_of(count, token_bytes, weight_bytes, channels):
    best = None
    for Q in range(1, count):
        if count % Q or channels % (Q * LANES):
            continue
        cost = token_bytes * Q + 2 * weight_bytes // Q
        if best is None or cost < best[0]:
            best = (cost, Q)
    return best[1]


def per_device(tokens, in_weight, short_filter, decay_rates, residues, skip_gain):
    N, T = lax.axis_size("ctx"), lax.axis_size("tp")
    R, D = tokens.shape
    depth, branches, channels = in_weight.shape
    modes = decay_rates.shape[0]
    Q = slices_of(N, R * T * D, depth * N * branches * channels, channels)
    H = N // Q
    C = channels // Q
    L = R * T
    M = Q * L
    groups = C // LANES
    G = max(1, min(PIECES, R // TAIL))
    dma = pltpu.SemaphoreType.DMA
    hbm = pl.BlockSpec(memory_space=pl.ANY)
    vmem = pl.BlockSpec(memory_space=pltpu.VMEM)
    f32, bf16 = jnp.float32, jnp.bfloat16
    return pl.pallas_call(
        functools.partial(fused_kernel, Q, N, T),
        out_shape=jax.ShapeDtypeStruct((L, channels), bf16),
        in_specs=[hbm, hbm, vmem, vmem, vmem, vmem],
        out_specs=hbm,
        scratch_shapes=[
            pltpu.VMEM((Q, T, R, D), bf16),
            pltpu.VMEM((groups, branches, N, depth, LANES), bf16),
            pltpu.VMEM((branches, M + SUBLANES, LANES), f32),
            pltpu.VMEM((groups, branches, TAIL, LANES), bf16),
            pltpu.VMEM((groups, branches, TAIL, LANES), bf16),
            pltpu.VMEM((M, LANES), f32),
            pltpu.VMEM((2, modes, SUBLANES, C), f32),
            pltpu.VMEM((modes, SUBLANES, LANES), f32),
            pltpu.VMEM((groups, modes, LANES), f32),
            pltpu.VMEM((groups, H, modes, LANES), f32),
            pltpu.VMEM((groups, Q, L, LANES), bf16),
            dma((Q * T, G)), dma((Q * T, G)), dma((N, groups + 1)), dma((N, groups + 1)),
            dma((groups, 2)), dma((groups, 2)), dma((groups, H)), dma((groups, H)),
            dma((groups, Q)), dma((groups, Q)), dma((2 * groups + 2,)),
        ],
        compiler_params=pltpu.CompilerParams(
            collective_id=0, has_side_effects=True, vmem_limit_bytes=VMEM_BYTES
        ),
        name="project_and_filter",
    )(tokens, in_weight.transpose(1, 0, 2), short_filter, decay_rates, residues, skip_gain[None])


def solution(mesh):
    in_specs = (
        P(("ctx", "tp"), None),
        P("ctx", None, "tp"),
        P(None, None, "tp"),
        P(None, "tp"),
        P(None, "tp"),
        P("tp"),
    )
    return jax.shard_map(
        per_device, mesh=mesh, in_specs=in_specs, out_specs=P("ctx", "tp"), check_vma=False
    )
```

```python
import functools

import jax
import jax.numpy as jnp
from jax import lax
from jax.experimental import pallas as pl
from jax.experimental.pallas import tpu as pltpu
from jax.sharding import PartitionSpec as P

MESH = pl.DeviceIdType.MESH
VMEM_BYTES = 60 * 1024 * 1024
SUBLANES = 8
TAIL = 16
PIECES = 2
LANES = 128
ROWS = 128


def bits_of(count):
    bits, bit = [], count // 2
    while bit:
        bits.append(bit)
        bit //= 2
    return bits


def flipped(index, mask):
    bit = 1
    while bit <= mask:
        if mask & bit:
            index = index + bit - 2 * bit * ((index // bit) % 2)
        bit *= 2
    return index


def fused_kernel(Q, N, T, tok_ref, w_ref, filt_ref, dec_ref, res_ref, skip_ref, out_ref,
                 tok, w, wid, tail, halo, prod, consts, st, seg, allseg, outbuf,
                 tok_send, tok_recv, w_send, w_recv, halo_send, halo_recv, seg_send, seg_recv,
                 out_send, out_recv, own_sem):
    ctx, t = lax.axis_index("ctx"), lax.axis_index("tp")
    H = N // Q
    h, q = ctx // Q, ctx % Q
    R = tok.shape[2]
    G = tok_send.shape[1]
    part_rows = R // G
    L = T * R
    M = Q * L
    groups, branches, depth = w.shape[0], w.shape[1], w.shape[3]
    C = groups * LANES
    modes, lags = dec_ref.shape[0], filt_ref.shape[1]
    steps = M // SUBLANES

    def remote(src, dst, send, recv, device):
        return pltpu.make_async_remote_copy(
            src_ref=src, dst_ref=dst, send_sem=send, recv_sem=recv, device_id=device, device_id_type=MESH
        )

    def lanes(owner, g):
        return pl.ds(pl.multiple_of(owner * C + g * LANES, LANES), LANES)

    parts = []
    for g in range(groups):
        if g < groups - 1:
            parts.append((g, 0, branches))
        else:
            parts.append((g, 1, branches))
            parts.append((g, 0, 1))
    P_count = len(parts)

    own_tok = pltpu.make_async_copy(tok_ref, tok.at[q, t], own_sem.at[P_count])

    def own_w(p):
        g, lo, hi = parts[p]
        return pltpu.make_async_copy(w_ref.at[lo:hi, :, lanes(q, g)], w.at[g, lo:hi, ctx], own_sem.at[p])

    own_tok.start()
    for p in range(P_count):
        own_w(p).start()
    allseg[...] = jnp.zeros(allseg.shape, jnp.float32)

    barrier = pltpu.get_barrier_semaphore()
    for mask in range(1, N):
        pl.semaphore_signal(barrier, inc=1, device_id=(flipped(ctx, mask), t), device_id_type=MESH)
    for bit in bits_of(T):
        pl.semaphore_signal(barrier, inc=1, device_id=(ctx, flipped(t, bit)), device_id_type=MESH)
    pl.semaphore_wait(barrier, N - 1 + len(bits_of(T)))

    levels = [(bit, 0) for bit in bits_of(Q)] + [(0, bit) for bit in bits_of(T)]

    def source_of(m):
        qm = sum(levels[k][0] for k in range(len(levels)) if m >> k & 1)
        tm = sum(levels[k][1] for k in range(len(levels)) if m >> k & 1)
        return flipped(q, qm), flipped(t, tm)

    def piece(m, g):
        a, b = source_of(m)
        return tok.at[a, b, pl.ds(g * part_rows, part_rows)]

    def tok_copy(m, k, g):
        src = piece(m, g) if m else tok_ref.at[pl.ds(g * part_rows, part_rows)]
        to = m + (1 << k)
        return remote(
            src, piece(m, g), tok_send.at[to, g], tok_recv.at[to, g],
            (flipped(ctx, levels[k][0]), flipped(t, levels[k][1])),
        )

    def tok_arrived(m, g):
        ref = piece(m, g)
        remote(ref, ref, own_sem.at[0], tok_recv.at[m, g], (ctx, t)).wait_recv()

    def w_copy(to, p):
        g, lo, hi = parts[p]
        return remote(
            w_ref.at[lo:hi, :, lanes(to % Q, g)], w.at[g, lo:hi, ctx], w_send.at[to, p], w_recv.at[ctx, p], (to, t)
        )

    def w_arrived(mask, p):
        g, lo, hi = parts[p]
        source = flipped(ctx, mask)
        ref = w.at[g, lo:hi, source]
        if mask:
            remote(ref, ref, own_sem.at[0], w_recv.at[source, p], (ctx, t)).wait_recv()
        else:
            own_w(p).wait()

    top = Q // 2
    side = max(top, 1)
    near = [[m for m in range(Q, N) if m & top and (m % side > 0) == turn] for turn in (False, True)]
    far = [[m for m in range(Q, N) if not m & top and (m % side > 0) == turn] for turn in (False, True)]
    inside = [[m for m in range(1, Q) if m & top and (m % side > 0) == turn] for turn in (False, True)]
    beside = [m for m in range(1, Q) if not m & top]
    middle = (ctx // Q + ctx // side) % 2 == 1
    end = jnp.logical_not(middle)

    from_middle = near[0] + inside[0] + near[1] + inside[1] + far[0] + far[1] + beside
    from_end = far[0] + far[1] + near[0] + near[1] + inside[0] + inside[1] + beside

    def send_some(p, here, masks):
        @pl.when(here)
        def _():
            for mask in masks:
                w_copy(flipped(ctx, mask), p).start()

    def send_w(p, inner=(True, False)):
        for here, masks in ((middle, from_middle), (end, from_end)):
            @pl.when(here)
            def _():
                for mask in masks:
                    if (mask < Q) in inner:
                        w_copy(flipped(ctx, mask), p).start()

    def halo_copy(g, lo, hi):
        return remote(
            tail.at[g, lo:hi], halo.at[g, lo:hi], halo_send.at[g, lo], halo_recv.at[g, lo], (ctx + Q, t)
        )

    def seg_copy(g, d):
        return remote(seg.at[g], allseg.at[g, h], seg_send.at[g, d], seg_recv.at[g, h], (ctx + d * Q, t))

    def out_copy(g, s):
        return remote(
            outbuf.at[g, s], out_ref.at[:, lanes(q, g)], out_send.at[g, s], out_recv.at[g, q], (h * Q + s, t)
        )

    def own_out(g):
        return pltpu.make_async_copy(outbuf.at[g, q], out_ref.at[:, lanes(q, g)], own_sem.at[P_count + 1 + g])

    for g in range(G):
        for k in range(len(levels)):
            tok_copy(0, k, g).start()
    send_w(0)

    dec = dec_ref[:, pl.ds(pl.multiple_of(q * C, LANES), C)]
    gain = res_ref[:, pl.ds(pl.multiple_of(q * C, LANES), C)] * jnp.sqrt(2.0 * dec)
    decay = jnp.exp(-dec)
    for m in range(modes):
        consts[0, m] = jnp.broadcast_to(decay[m : m + 1], (SUBLANES, C))
        consts[1, m] = jnp.broadcast_to(gain[m : m + 1], (SUBLANES, C))

    def forward(*some, pieces=range(G)):
        for g in pieces:
            for m in some:
                tok_arrived(m, g)
                for k in range(m.bit_length(), len(levels)):
                    tok_copy(m, k, g).start()

    def by_hops(count):
        return sorted(range(count), key=lambda m: (bin(m).count("1"), m))

    def rounded(value):
        return value.astype(jnp.bfloat16).astype(jnp.float32)

    def project_shard(g, lo, hi, s):
        a = tok.at[s].reshape(L, N * depth)
        b = [w.at[g, j].reshape(N * depth, LANES)[...] for j in range(lo, hi)]
        b = jnp.concatenate(b, axis=1) if len(b) > 1 else b[0]
        value = jnp.dot(a[...], b, preferred_element_type=jnp.float32)
        at = pl.ds(pl.multiple_of(SUBLANES + s * L, SUBLANES), L)
        for j in range(lo, hi):
            wid[j, at] = rounded(value[:, (j - lo) * LANES : (j - lo + 1) * LANES])

    def project_piece(g, lo, hi, part, first, last):
        b = [w.at[g, j, pl.ds(part * Q, Q)].reshape(Q * depth, LANES) for j in range(lo, hi)]

        @pl.loop(0, Q)
        def _(s):
            a = tok.at[s].reshape(L, N * depth)[:, pl.ds(pl.multiple_of(part * Q * depth, LANES), Q * depth)]
            c = [ref[...] for ref in b]
            c = jnp.concatenate(c, axis=1) if len(c) > 1 else c[0]
            value = jnp.dot(a, c, preferred_element_type=jnp.float32)
            at = pl.ds(pl.multiple_of(SUBLANES + s * L, SUBLANES), L)
            for j in range(lo, hi):
                add = value[:, (j - lo) * LANES : (j - lo + 1) * LANES]
                add = add if first else wid[j, at] + add
                wid[j, at] = rounded(add) if last else add

    def send_tail(g, lo, hi):
        for j in range(lo, hi):
            tail[g, j] = wid[j, SUBLANES + M - TAIL : SUBLANES + M].astype(jnp.bfloat16)

        @pl.when(h + 1 < H)
        def _():
            halo_copy(g, lo, hi).start()

    def take_halo(g, lo, hi):
        @pl.when(h == 0)
        def _():
            for j in range(lo, hi):
                wid[j, 0:SUBLANES] = jnp.zeros((SUBLANES, LANES), jnp.float32)

        @pl.when(h > 0)
        def _():
            if g == groups - 1:
                halo_copy(g, lo, hi).wait_recv()
            elif lo == 1:
                halo_copy(g, 0, branches).wait_recv()
            for j in range(lo, hi):
                wid[j, 0:SUBLANES] = halo[g, j].astype(jnp.float32)[TAIL - SUBLANES :]

    def features(g, j, start):
        total = None
        for o in range(lags):
            term = filt_ref[j, o : o + 1, lanes(q, g)] * wid[j, pl.ds(start + (SUBLANES - o), ROWS)]
            total = term if total is None else total + term
        return total

    def gather_states(g):
        @pl.loop(0, M // ROWS)
        def _(r):
            start = pl.multiple_of(r * ROWS, ROWS)
            prod[pl.ds(start, ROWS)] = features(g, 1, start) * features(g, 2, start)

        cols = slice(g * LANES, (g + 1) * LANES)
        factor = [consts[0, m, :, cols] for m in range(modes)]

        def gather(i, state):
            v = prod[pl.ds(i, SUBLANES, stride=steps), :]
            return tuple(f * s + v for f, s in zip(factor, state))

        zero = jnp.zeros((SUBLANES, LANES), jnp.float32)
        state = lax.fori_loop(0, steps, gather, (zero,) * modes, unroll=16)
        for m in range(modes):
            st[m] = state[m]
        rate = dec_ref[:, lanes(q, g)]
        sub_decay = jnp.exp(-rate * steps)
        e = jnp.zeros((modes, LANES), jnp.float32)
        for c in range(SUBLANES):
            e = sub_decay * e + st[:, c, :]
        seg[g] = e
        for d in range(1, H):
            @pl.when(h + d < H)
            def _():
                seg_copy(g, d).start()

    def convolve(g):
        cols = slice(g * LANES, (g + 1) * LANES)
        rate = dec_ref[:, lanes(q, g)]
        sub_decay = jnp.exp(-rate * steps)
        whole = jnp.exp(-rate * M)
        for d in range(H - 1):
            @pl.when(d < h)
            def _():
                ref = allseg.at[g, d]
                remote(ref, ref, own_sem.at[0], seg_recv.at[g, d], (ctx, t)).wait_recv()
        e = jnp.zeros((modes, LANES), jnp.float32)
        for d in range(H - 1):
            e = jnp.where(d < h, whole * e + allseg[g, d], e)
        for c in range(SUBLANES):
            now = st[:, c, :]
            st[:, c, :] = e
            e = sub_decay * e + now
        direct = jnp.broadcast_to(skip_ref[:, lanes(q, g)], (SUBLANES, LANES))

        def step(i, state):
            at = pl.ds(i, SUBLANES, stride=steps)
            v = prod[at, :]
            state = tuple(consts[0, m, :, cols] * s + v for m, s in enumerate(state))
            terms = [consts[1, m, :, cols] * s for m, s in enumerate(state)]
            terms.append(direct * v)
            while len(terms) > 1:
                terms = [a + b for a, b in zip(terms[::2], terms[1::2])] + (
                    [terms[-1]] if len(terms) % 2 else []
                )
            prod[at, :] = terms[0]
            return state

        lax.fori_loop(0, steps, step, tuple(st[m] for m in range(modes)), unroll=16)

    def finish(g):
        for s in range(Q - 1, -1, -1):
            if s == 0:
                take_halo(g, 0, 1)

            @pl.loop(0, L // ROWS)
            def _(r):
                start = pl.multiple_of(s * L + r * ROWS, ROWS)
                inner = pl.multiple_of(r * ROWS, ROWS)
                value = features(g, 0, start) * prod[pl.ds(start, ROWS)]
                outbuf[g, s, pl.ds(inner, ROWS)] = value.astype(outbuf.dtype)

            @pl.when(s != q)
            def _():
                out_copy(g, s).start()

            @pl.when(s == q)
            def _():
                own_out(g).start()

    last = groups - 1
    shards = by_hops(Q)
    forward(*[m for m in shards if bin(m).count("1") == 1])
    if P_count > 1:
        send_some(1, middle, far[0] + far[1])
        send_some(1, end, inside[0] + inside[1] + far[0] + far[1])
    early = shards[:-1] if Q > 2 else shards
    late = shards[len(early) :]
    half = G // 2 if late else 0
    for m in shards:
        if m & (m - 1):
            forward(m, pieces=range(half))
    if P_count > 1:
        send_some(1, middle, near[0] + near[1] + inside[0] + inside[1] + beside)
        send_some(1, end, near[0] + near[1] + beside)
    for sm in early:
        for tm in by_hops(T)[1:]:
            forward(sm + Q * tm)
    for m in shards:
        if m & (m - 1):
            forward(m, pieces=range(half, G))
    own_tok.wait()

    def project_first(sm):
        shard = q
        for k, (bit, _) in enumerate(levels):
            if sm >> k & 1:
                shard = flipped(shard, bit)
        project_shard(0, 1, branches, shard)
        project_shard(0, 0, 1, shard)

    if last:
        for mask in range(N):
            w_arrived(mask, 0)
        for sm in early:
            project_first(sm)
    for sm in late:
        for tm in by_hops(T)[1:]:
            forward(sm + Q * tm)
        if last:
            project_first(sm)

    for p in range(2, P_count):
        send_w(p, (True,))

    def project_last(p, part):
        for mask in range(part * Q, part * Q + Q):
            w_arrived(mask, p)
        g, lo, hi = parts[p]
        project_piece(g, lo, hi, flipped(h, part), part == 0, part == H - 1)

    for g in range(last):
        if g:
            for mask in range(N):
                w_arrived(mask, g)

            @pl.loop(0, Q)
            def _(s):
                project_shard(g, 1, branches, s)
                project_shard(g, 0, 1, s)
        send_tail(g, 0, branches)
        take_halo(g, 1, branches)
        gather_states(g)
        if g == last - 1:
            project_last(P_count - 2, 0)
        if g == last - 1:
            for p in range(2, P_count):
                send_some(p, middle, far[0] + far[1])
        convolve(g)
        finish(g)
    for p in range(2, P_count):
        send_some(p, middle, near[0] + near[1])
        send_some(p, end, far[0] + far[1] + near[0] + near[1])
    for part in range(1 if last else 0, H):
        project_last(P_count - 2, part)
    send_tail(last, 1, branches)
    take_halo(last, 1, branches)
    gather_states(last)
    project_last(P_count - 1, 0)
    convolve(last)
    for part in range(1, H):
        project_last(P_count - 1, part)
    send_tail(last, 0, 1)
    finish(last)

    for m in range(1 << len(levels)):
        for k in range(m.bit_length(), len(levels)):
            for g in range(G):
                tok_copy(m, k, g).wait_send()
    for p in range(P_count):
        for mask in range(1, N):
            w_copy(flipped(ctx, mask), p).wait_send()
    for g in range(groups):
        @pl.when(h + 1 < H)
        def _():
            if g < groups - 1:
                halo_copy(g, 0, branches).wait_send()
            else:
                halo_copy(g, 0, 1).wait_send()
                halo_copy(g, 1, branches).wait_send()
        for d in range(1, H):
            @pl.when(h + d < H)
            def _():
                seg_copy(g, d).wait_send()
        own_out(g).wait()
        for s in range(Q):
            @pl.when(s != q)
            def _():
                out_copy(g, s).wait_send()
                ref = out_ref.at[:, lanes(s, g)]
                remote(outbuf.at[g, s], ref, own_sem.at[0], out_recv.at[g, s], (ctx, t)).wait_recv()


def slices_of(count, token_bytes, weight_bytes, channels):
    best = None
    for Q in range(1, count):
        if count % Q or channels % (Q * LANES):
            continue
        cost = token_bytes * Q + 2 * weight_bytes // Q
        if best is None or cost < best[0]:
            best = (cost, Q)
    return best[1]


def per_device(tokens, in_weight, short_filter, decay_rates, residues, skip_gain):
    N, T = lax.axis_size("ctx"), lax.axis_size("tp")
    R, D = tokens.shape
    depth, branches, channels = in_weight.shape
    modes = decay_rates.shape[0]
    Q = slices_of(N, R * T * D, depth * N * branches * channels, channels)
    H = N // Q
    C = channels // Q
    L = R * T
    M = Q * L
    groups = C // LANES
    G = max(1, min(PIECES, R // TAIL))
    dma = pltpu.SemaphoreType.DMA
    hbm = pl.BlockSpec(memory_space=pl.ANY)
    vmem = pl.BlockSpec(memory_space=pltpu.VMEM)
    f32, bf16 = jnp.float32, jnp.bfloat16
    return pl.pallas_call(
        functools.partial(fused_kernel, Q, N, T),
        out_shape=jax.ShapeDtypeStruct((L, channels), bf16),
        in_specs=[hbm, hbm, vmem, vmem, vmem, vmem],
        out_specs=hbm,
        scratch_shapes=[
            pltpu.VMEM((Q, T, R, D), bf16),
            pltpu.VMEM((groups, branches, N, depth, LANES), bf16),
            pltpu.VMEM((branches, M + SUBLANES, LANES), f32),
            pltpu.VMEM((groups, branches, TAIL, LANES), bf16),
            pltpu.VMEM((groups, branches, TAIL, LANES), bf16),
            pltpu.VMEM((M, LANES), f32),
            pltpu.VMEM((2, modes, SUBLANES, C), f32),
            pltpu.VMEM((modes, SUBLANES, LANES), f32),
            pltpu.VMEM((groups, modes, LANES), f32),
            pltpu.VMEM((groups, H, modes, LANES), f32),
            pltpu.VMEM((groups, Q, L, LANES), bf16),
            dma((Q * T, G)), dma((Q * T, G)), dma((N, groups + 1)), dma((N, groups + 1)),
            dma((groups, 2)), dma((groups, 2)), dma((groups, H)), dma((groups, H)),
            dma((groups, Q)), dma((groups, Q)), dma((2 * groups + 2,)),
        ],
        compiler_params=pltpu.CompilerParams(
            collective_id=0, has_side_effects=True, vmem_limit_bytes=VMEM_BYTES
        ),
        name="project_and_filter",
    )(tokens, in_weight.transpose(1, 0, 2), short_filter, decay_rates, residues, skip_gain[None])


def solution(mesh):
    in_specs = (
        P(("ctx", "tp"), None),
        P("ctx", None, "tp"),
        P(None, None, "tp"),
        P(None, "tp"),
        P(None, "tp"),
        P("tp"),
    )
    return jax.shard_map(
        per_device, mesh=mesh, in_specs=in_specs, out_specs=P("ctx", "tp"), check_vma=False
    )
```
